32 devices in a mesh: width: 4 (over y, core), hidden: 8 (over z, x).
Axes of the slice: x: 2, y: 2, z: 4, core: 2. Of those that a mesh axis runs over, the one named last changes fastest.
Arguments:
- start_latent: float32 [512, 6144], P(None, 'width'), may hold values from -6 to 6
- target_one: float32 [512, 6144], P(None, 'width'), may hold values from -6 to 6
- target_two: float32 [512, 6144], P(None, 'width'), may hold values from -6 to 6
- w_up: bfloat16 [6144, 24576], P('width', 'hidden'), may hold values from -0.078125 to 0.078125
- w_down: bfloat16 [24576, 6144], P('hidden', 'width'), may hold values from -0.0390625 to 0.0390625
Outputs:
- grad_start: float32 [512, 6144], P('hidden', 'width')
- grad_up: float32 [6144, 24576], P('width', 'hidden')
- grad_down: float32 [24576, 6144], P('hidden', 'width')
The draws below stay inside these ranges and needn't reach their ends.
All inputs are finite; a program needn't handle non-finite values.
Results may differ from the reference program's by a relative error of at most 0.018.
Values may be sent and summed in bfloat16 or wider, within the bound.
A program may use at most 192 MiB of HBM per device.

```python
import math
import jax
import jax.numpy as jnp
from jax import lax

D = 6144
FF = 24576
ROWS = 512
N_WIDTH = 4


def block_levels(key, shape, cuts, least, largest):
    def one(position, blocks):
        heights = jax.random.uniform(jax.random.fold_in(jax.random.fold_in(key, 6), position), (blocks,), jnp.float32, least / len(cuts), largest / len(cuts))
        return jnp.repeat(jnp.exp(heights), shape[position] // blocks).reshape((-1,) + (1,) * (len(shape) - position - 1))

    loudness = one(*cuts[0])
    for cut in cuts[1:]:
        loudness = loudness * one(*cut)
    return loudness


def noise(key, shape, width, reach, shards=(), kind=jnp.bfloat16):
    entries = width * jax.random.normal(key, shape, jnp.float32)
    if shards:
        entries = entries * block_levels(key, shape, shards, -0.22, 0.18)
    return jnp.clip(entries, -reach, reach).astype(kind)


def setup_inputs(seed: int = 0) -> dict:
    seeds = jax.random.split(jax.random.key(seed), 6)
    start_latent = noise(seeds[0], (ROWS, D), 1.0, 6.0, ((1, 4),), jnp.float32)
    target_one = noise(seeds[1], (ROWS, D), 1.0, 6.0, ((1, 4),), jnp.float32)
    target_two = noise(seeds[2], (ROWS, D), 1.0, 6.0, ((1, 4),), jnp.float32)
    w_up = noise(seeds[3], (D, FF), D ** -0.5, 0.078125, ((0, 4), (1, 8)))
    w_down = noise(seeds[4], (FF, D), FF ** -0.5, 0.0390625, ((0, 8), (1, 4)))
    return dict(start_latent=start_latent, target_one=target_one, target_two=target_two, w_up=w_up, w_down=w_down)


gelu_scale = math.sqrt(2.0 / math.pi)
cubic_coef = 0.044715

def gelu_parts(preact):
    inner = gelu_scale * (preact + cubic_coef * preact * preact * preact)
    tangent = jnp.tanh(inner)
    value_out = 0.5 * preact * (1.0 + tangent)
    slope_out = 0.5 * (1.0 + tangent) + 0.5 * preact * (1.0 - tangent * tangent) * gelu_scale * (1.0 + 3.0 * cubic_coef * preact * preact)
    return (value_out, slope_out)

def block_sum(left_mat, right_mat, right_rows):
    block_width = left_mat.shape[1] // N_WIDTH
    summed = jnp.zeros((left_mat.shape[0], right_mat.shape[1] if right_rows else right_mat.shape[0]), jnp.float32)

    def add_block(accum, block_index):
        first_col = (block_index * block_width).astype(jnp.int32)
        left_cols = lax.dynamic_slice_in_dim(left_mat, first_col, block_width, 1)
        if right_rows:
            right_part = lax.dynamic_slice_in_dim(right_mat, first_col, block_width, 0)
            product = jnp.dot(left_cols, right_part, preferred_element_type=jnp.float32)
        else:
            right_part = lax.dynamic_slice_in_dim(right_mat, first_col, block_width, 1)
            product = jnp.dot(left_cols, right_part.T, preferred_element_type=jnp.float32)
        rounded = lax.optimization_barrier(product.astype(jnp.bfloat16))
        return (accum + rounded.astype(jnp.float32), None)
    summed, unused = lax.scan(add_block, summed, jnp.arange(N_WIDTH, dtype=jnp.int32))
    return summed

def reference(start_latent, target_one, target_two, w_up, w_down):
    input_zero = start_latent.astype(jnp.bfloat16)
    pre_zero = block_sum(input_zero, w_up, True).astype(jnp.bfloat16)
    gelu_zero, slope_zero = gelu_parts(pre_zero.astype(jnp.float32))
    act_zero = gelu_zero.astype(jnp.bfloat16)
    latent_one = start_latent + jnp.dot(act_zero, w_down, preferred_element_type=jnp.float32)
    input_one = latent_one.astype(jnp.bfloat16)
    pre_one = block_sum(input_one, w_up, True).astype(jnp.bfloat16)
    gelu_one, slope_one = gelu_parts(pre_one.astype(jnp.float32))
    act_one = gelu_one.astype(jnp.bfloat16)
    error_two = target_two.astype(jnp.bfloat16)
    back_one = block_sum(error_two, w_down, False).astype(jnp.bfloat16)
    inner_one = (back_one.astype(jnp.float32) * slope_one).astype(jnp.bfloat16)
    grad_one = target_one + target_two + jnp.dot(inner_one, w_up.T, preferred_element_type=jnp.float32)
    error_one = grad_one.astype(jnp.bfloat16)
    back_zero = block_sum(error_one, w_down, False).astype(jnp.bfloat16)
    inner_zero = (back_zero.astype(jnp.float32) * slope_zero).astype(jnp.bfloat16)
    grad_start = grad_one + jnp.dot(inner_zero, w_up.T, preferred_element_type=jnp.float32)
    grad_up = jnp.dot(input_zero.T, inner_zero, preferred_element_type=jnp.float32) + jnp.dot(input_one.T, inner_one, preferred_element_type=jnp.float32)
    grad_down = jnp.dot(act_zero.T, error_one, preferred_element_type=jnp.float32) + jnp.dot(act_one.T, error_two, preferred_element_type=jnp.float32)
    return (grad_start, grad_up, grad_down)
```

```python
import functools
import math

import jax
import jax.numpy as jnp
from jax import lax
from jax.experimental import pallas as pl
from jax.experimental.pallas import tpu as pltpu
from jax.sharding import PartitionSpec as P

gelu_scale = math.sqrt(2.0 / math.pi)
cubic_coef = 0.044715
CHUNKS = 2
OFFSET = 2
F32, BF16 = jnp.float32, jnp.bfloat16
NT = (((1,), (1,)), ((), ()))


def gelu_parts(preact):
    square = preact * preact
    tangent = jnp.tanh(gelu_scale * (preact + cubic_coef * square * preact))
    half = 0.5 * (1.0 + tangent)
    slope_out = half + 0.5 * preact * (1.0 - tangent * tangent) * (
        gelu_scale + 3.0 * cubic_coef * gelu_scale * square
    )
    return (preact * half, slope_out)


def tile_of(size):
    for tile in (512, 384, 256, 128):
        if size % tile == 0:
            return tile
    return size


def plan(mesh_width, mesh_hidden, rows):
    hmaj = 4 if mesh_hidden % 4 == 0 else 1
    share = rows // mesh_hidden
    chunks = max(1, min(CHUNKS, share // 16))
    return hmaj, mesh_hidden // hmaj, chunks, share // chunks


def kernel(
    dims, x0_in, e2_in, st_own, t_own, wu_in, wd_in,
    xs_o, err_o, act_o, inn_o, gs_o,
    wu, wd, xs, err, act, inn, bk0, snd, rcv, own, yrc, hp, xr, zs, zr, gone,
    in_sem, out_sem, c1_s, c1_r, y_s, y_r, c3_s, c3_r,
    x_s, x_r, z_s, z_r, az_s, az_r, ax_s, ax_r,
):
    wide, hmaj, hmin, chunks, r = dims
    ysize = wide // 2
    rows, d = x0_in.shape
    f = wu_in.shape[1]
    fh = f // 2
    big = rows // chunks
    xrows = hmaj * r
    w = lax.axis_index("width")
    core, y = w % 2, w // 2
    h = lax.axis_index("hidden")
    hx, hz = h % hmin, h // hmin
    core_peer = {"width": y * 2 + 1 - core}

    def y_peer(j):
        return {"width": ((y + j) % ysize) * 2 + core}

    def x_pos(j):
        return (hx + j) % hmin

    def z_pos(j):
        return (hz + j) % hmaj

    def x_peer(j):
        return {"hidden": hz * hmin + x_pos(j)}

    def z_peer(j):
        return {"hidden": z_pos(j) * hmin + hx}

    loads = [
        pltpu.make_async_copy(src, dst, in_sem.at[i])
        for i, (src, dst) in enumerate(
            [
                (x0_in, xs.at[pl.ds(0, rows)]),
                (wu_in, wu),
                (wd_in, wd),
                (e2_in, err.at[pl.ds(rows, rows)]),
            ]
        )
    ]
    for load in loads:
        load.start()

    barrier = pltpu.get_barrier_semaphore()
    peers = [core_peer] + [y_peer(j) for j in range(1, ysize)]
    peers += [x_peer(j) for j in range(1, hmin)] + [z_peer(j) for j in range(1, hmaj)]
    for peer in peers:
        pl.semaphore_signal(barrier, inc=1, device_id=peer, device_id_type=pl.DeviceIdType.MESH)
    pl.semaphore_wait(barrier, len(peers))

    loaded = set()

    def need(*which):
        for i in which:
            if i not in loaded:
                loaded.add(i)
                loads[i].wait()

    inflight = {}

    def send(key, src, dst, ssem, rsem, peer):
        copy = pltpu.make_async_remote_copy(
            src_ref=src, dst_ref=dst, send_sem=ssem, recv_sem=rsem,
            device_id=peer, device_id_type=pl.DeviceIdType.MESH,
        )
        copy.start()
        inflight.setdefault(key, []).append(copy)

    def wait(key):
        for copy in inflight.pop(key, []):
            copy.wait()

    outs = []

    def put(src, dst):
        copy = pltpu.make_async_copy(src, dst, out_sem.at[len(outs)])
        copy.start()
        outs.append(copy)

    def put_wide(buf, out, first, count):
        for k in range(2):
            put(buf.at[k, pl.ds(first, count)], out.at[pl.ds(first, count), pl.ds(k * fh, fh)])

    ntile = tile_of(fh)
    dtile = tile_of(d)

    def half_matmul(lhs, lrow, weight, half, dst, row):
        def body(t, carry):
            col = pl.multiple_of(half * fh + t * ntile, 128)
            left = lhs[pl.ds(lrow, big), :]
            if weight == "up":
                prod = jnp.dot(left, wu[:, pl.ds(col, ntile)], preferred_element_type=F32)
            else:
                prod = lax.dot_general(left, wd[pl.ds(col, ntile), :], NT, preferred_element_type=F32)
            dst[pl.ds(row, big), pl.ds(pl.multiple_of(t * ntile, 128), ntile)] = prod.astype(BF16)
            return carry

        lax.fori_loop(0, fh // ntile, body, 0)

    lefts = [(xs, 0, "up"), (xs, rows, "up"), (err, rows, "down"), (err, 0, "down")]
    dests = [(inn, 0), (inn, rows), (act, rows), (bk0, 0)]
    sets = [0, 0, 1, 0]

    def w1(ar, c):
        lhs, base, weight = lefts[ar]
        need(*{0: (0, 1), 1: (), 2: (2, 3), 3: ()}[ar])
        if ar == 1:
            wait(("ax", 0, c))
            put(xs.at[pl.ds(rows + c * big, big)], xs_o.at[pl.ds(rows + c * big, big)])
        if ar == 3:
            wait(("ax", 1, c))
            put(err.at[pl.ds(c * big, big)], err_o.at[pl.ds(c * big, big)])
        s, row = sets[ar], c * big
        half_matmul(lhs, base + row, weight, 1 - core, snd.at[s], row)
        send(("c1", ar, c), snd.at[s, pl.ds(row, big)], rcv.at[s, pl.ds(row, big)],
             c1_s.at[ar, c], c1_r.at[ar, c], core_peer)
        half_matmul(lhs, base + row, weight, core, own.at[s], row)

    def row_loop(count, step, body):
        def wrapped(i, carry):
            body(pl.multiple_of(i * step, step))
            return carry

        lax.fori_loop(0, count // step, wrapped, 0)

    def w2(ar, c):
        s, row = sets[ar], c * big
        wait(("c1", ar, c))

        def body(i):
            at = pl.ds(row + i, 16)
            own[s, at] = (own[s, at].astype(F32) + rcv[s, at].astype(F32)).astype(BF16)

        row_loop(big, 16, body)
        dst, base = dests[ar]
        for j in range(1, ysize):
            if ysize == 2:
                target = dst.at[core, pl.ds(base + row, big)]
            else:
                target = yrc.at[ar * ysize + j, pl.ds(row, big)]
            send(("y", ar, c), own.at[s, pl.ds(row, big)], target,
                 y_s.at[ar, c, j], y_r.at[ar, c, j], y_peer(j))

    def w3(ar, c):
        s, row = sets[ar], c * big
        wait(("y", ar, c))
        dst, base = dests[ar]

        def body(i):
            at = pl.ds(row + i, 16)
            to = pl.ds(base + row + i, 16)
            total = own[s, at].astype(F32)
            for j in range(1, ysize):
                got = dst[core, to] if ysize == 2 else yrc[ar * ysize + j, at]
                total = total + got.astype(F32)
            dst[core, to] = total.astype(BF16)

        row_loop(big, 16, body)
        place = dst.at[core, pl.ds(base + row, big)]
        send(("c3", ar, c), place, place, c3_s.at[ar, c], c3_r.at[ar, c], core_peer)

    def h1(st, c):
        row = c * big
        wait(("c3", (0, 1, 3)[st], c))
        if st == 0:
            need(2)
        if st == 1:
            wait(("c3", 2, c))
        for k in range(2):
            def body(i):
                a = pl.ds(row + i, 16)
                b = pl.ds(rows + row + i, 16)
                if st == 0:
                    value, slope = gelu_parts(inn[k, a].astype(F32))
                    act[k, a] = value.astype(BF16)
                    inn[k, a] = slope.astype(BF16)
                elif st == 1:
                    value, slope = gelu_parts(inn[k, b].astype(F32))
                    back = act[k, b].astype(F32)
                    act[k, b] = value.astype(BF16)
                    inn[k, b] = (back * slope).astype(BF16)
                else:
                    inn[k, a] = (bk0[k, a].astype(F32) * inn[k, a].astype(F32)).astype(BF16)

            row_loop(big, 16, body)
        base = rows if st == 1 else 0

        def mm(t, carry):
            col = pl.ds(pl.multiple_of(t * dtile, 128), dtile)
            total = None
            for k in range(2):
                if st == 0:
                    prod = jnp.dot(act[k, pl.ds(row, big)], wd[pl.ds(k * fh, fh), col],
                                   preferred_element_type=F32)
                else:
                    prod = lax.dot_general(inn[k, pl.ds(base + row, big)], wu[col, pl.ds(k * fh, fh)],
                                           NT, preferred_element_type=F32)
                total = prod if total is None else total + prod
            hp[pl.ds(row, big), col] = total.astype(BF16)
            return carry

        lax.fori_loop(0, d // dtile, mm, 0)
        if st == 0:
            put_wide(act, act_o, row, big)
        elif st == 1:
            put_wide(act, act_o, rows + row, big)
            put_wide(inn, inn_o, rows + row, big)
        else:
            put_wide(inn, inn_o, row, big)
        for j in range(1, hmin):
            src = pl.ds(pl.multiple_of(row + x_pos(j) * xrows, 8), xrows)
            send(("x", st, c), hp.at[src], xr.at[j, pl.ds(c * xrows, xrows)],
                 x_s.at[st, c, j], x_r.at[st, c, j], x_peer(j))

    def h2(st, c):
        wait(("x", st, c))

        def body(i):
            at = pl.ds(c * xrows + i, 16)
            mine = pl.ds(pl.multiple_of(c * big + hx * xrows + i, 16), 16)
            total = hp[mine, :].astype(F32)
            for j in range(1, hmin):
                total = total + xr[j, at].astype(F32)
            zs[at] = total.astype(BF16)

        row_loop(xrows, 16, body)
        for j in range(1, hmaj):
            src = pl.ds(pl.multiple_of(c * xrows + z_pos(j) * r, 16), r)
            send(("z", st, c), zs.at[src], zr.at[j, pl.ds(c * r, r)],
                 z_s.at[st, c, j], z_r.at[st, c, j], z_peer(j))

    def share_place(st, c):
        buf, base = ((xs, rows), (err, 0))[st]
        return buf, base + c * big + hx * xrows

    def h3(st, c):
        wait(("z", st, c))
        for i in range(0, r, 16):
            at = pl.ds(c * r + i, 16)
            total = zs[pl.ds(pl.multiple_of(c * xrows + hz * r + i, 16), 16), :].astype(F32)
            for j in range(1, hmaj):
                total = total + zr[j, at].astype(F32)
            if st == 2:
                gs_o[at] = gone[at] + total
                continue
            total = total + (st_own, t_own)[st][at]
            if st == 1:
                gone[at] = total
            buf, first = share_place(st, c)
            buf[pl.ds(pl.multiple_of(first + hz * r + i, 16), 16), :] = total.astype(BF16)
        if st < 2:
            buf, first = share_place(st, c)
            place = buf.at[pl.ds(pl.multiple_of(first + hz * r, 16), r)]
            for j in range(1, hmaj):
                send(("az", st, c), place, place, az_s.at[st, c, j], az_r.at[st, c, j], z_peer(j))

    def h4(st, c):
        wait(("az", st, c))
        buf, first = share_place(st, c)
        place = buf.at[pl.ds(pl.multiple_of(first, 16), xrows)]
        for j in range(1, hmin):
            send(("ax", st, c), place, place, ax_s.at[st, c, j], ax_r.at[st, c, j], x_peer(j))

    need(0)
    put(xs.at[pl.ds(0, rows)], xs_o.at[pl.ds(0, rows)])
    chain = [
        (w1, 0), (w2, 0), (w3, 0), (h1, 0), (w1, 2), (h2, 0), (w2, 2), (h3, 0), (w3, 2), (h4, 0),
        (w1, 1), (w2, 1), (w3, 1), (h1, 1), (h2, 1), (h3, 1), (h4, 1),
        (w1, 3), (w2, 3), (w3, 3), (h1, 2), (h2, 2), (h3, 2),
    ]
    order = sorted(
        (i + c * OFFSET, c, i) for i in range(len(chain)) for c in range(chunks)
    )
    for _, c, i in order:
        step, arg = chain[i]
        step(arg, c)
    need(3)
    put(err.at[pl.ds(rows, rows)], err_o.at[pl.ds(rows, rows)])
    for copy in outs:
        copy.wait()


def shards(wide, hidden, start_latent, target_one, target_two, w_up, w_down):
    rows, d = start_latent.shape
    f = w_up.shape[1]
    hmaj, hmin, chunks, r = plan(wide, hidden, rows)
    share = rows // hidden
    ysize = wide // 2
    fh = f // 2
    xrows_all = rows // hmin

    def reorder(arr):
        cut = arr.astype(BF16).reshape(hmaj, hmin, chunks, r, d)
        return cut.transpose(2, 1, 0, 3, 4).reshape(rows, d)

    first = lax.axis_index("hidden") * share
    st_own = lax.dynamic_slice_in_dim(start_latent, first, share, 0)
    t_own = lax.dynamic_slice_in_dim(target_one, first, share, 0) + lax.dynamic_slice_in_dim(
        target_two, first, share, 0
    )
    vmem = pl.BlockSpec(memory_space=pltpu.VMEM)
    hbm = pl.BlockSpec(memory_space=pl.ANY)
    dma = pltpu.SemaphoreType.DMA
    yslots = 4 * ysize if ysize > 2 else 1
    yrows = rows if ysize > 2 else 16
    xs, err, act, inn, grad_start = pl.pallas_call(
        functools.partial(kernel, (wide, hmaj, hmin, chunks, r)),
        out_shape=(
            jax.ShapeDtypeStruct((2 * rows, d), BF16),
            jax.ShapeDtypeStruct((2 * rows, d), BF16),
            jax.ShapeDtypeStruct((2 * rows, f), BF16),
            jax.ShapeDtypeStruct((2 * rows, f), BF16),
            jax.ShapeDtypeStruct((share, d), F32),
        ),
        in_specs=[hbm, hbm, vmem, vmem, hbm, hbm],
        out_specs=[hbm, hbm, hbm, hbm, vmem],
        scratch_shapes=[
            pltpu.VMEM((d, f), BF16),
            pltpu.VMEM((f, d), BF16),
            pltpu.VMEM((2 * rows, d), BF16),
            pltpu.VMEM((2 * rows, d), BF16),
            pltpu.VMEM((2, 2 * rows, fh), BF16),
            pltpu.VMEM((2, 2 * rows, fh), BF16),
            pltpu.VMEM((2, rows, fh), BF16),
            pltpu.VMEM((2, rows, fh), BF16),
            pltpu.VMEM((2, rows, fh), BF16),
            pltpu.VMEM((2, rows, fh), BF16),
            pltpu.VMEM((yslots, yrows, fh if ysize > 2 else 128), BF16),
            pltpu.VMEM((rows, d), BF16),
            pltpu.VMEM((hmin, xrows_all, d), BF16),
            pltpu.VMEM((xrows_all, d), BF16),
            pltpu.VMEM((hmaj, share, d), BF16),
            pltpu.VMEM((share, d), F32),
            dma((4,)),
            dma((2 + 10 * chunks,)),
            dma((4, chunks)),
            dma((4, chunks)),
            dma((4, chunks, ysize)),
            dma((4, chunks, ysize)),
            dma((4, chunks)),
            dma((4, chunks)),
            dma((3, chunks, hmin)),
            dma((3, chunks, hmin)),
            dma((3, chunks, hmaj)),
            dma((3, chunks, hmaj)),
            dma((2, chunks, hmaj)),
            dma((2, chunks, hmaj)),
            dma((2, chunks, hmin)),
            dma((2, chunks, hmin)),
        ],
        compiler_params=pltpu.CompilerParams(
            collective_id=0, has_side_effects=True, vmem_limit_bytes=67043328
        ),
    )(reorder(start_latent), reorder(target_two), st_own, t_own, w_up, w_down)
    over_rows = (((0,), (0,)), ((), ()))
    grad_up = lax.dot_general(xs, inn, over_rows, preferred_element_type=F32)
    grad_down = lax.dot_general(act, err, over_rows, preferred_element_type=F32)
    return (grad_start, grad_up, grad_down)


def solution(mesh):
    return jax.shard_map(
        functools.partial(shards, mesh.shape["width"], mesh.shape["hidden"]),
        mesh=mesh,
        in_specs=(
            P(None, "width"),
            P(None, "width"),
            P(None, "width"),
            P("width", "hidden"),
            P("hidden", "width"),
        ),
        out_specs=(P("hidden", "width"), P("width", "hidden"), P("hidden", "width")),
        check_vma=False,
    )
```

```python
import functools
import math

import jax
import jax.numpy as jnp
from jax import lax
from jax.experimental import pallas as pl
from jax.experimental.pallas import tpu as pltpu
from jax.sharding import PartitionSpec as P

gelu_scale = math.sqrt(2.0 / math.pi)
cubic_coef = 0.044715
CHUNKS = 4
OFFSET = 1
F32, BF16 = jnp.float32, jnp.bfloat16
NT = (((1,), (1,)), ((), ()))


def gelu_parts(preact):
    square = preact * preact
    tangent = jnp.tanh(gelu_scale * (preact + cubic_coef * square * preact))
    half = 0.5 * (1.0 + tangent)
    slope_out = half + 0.5 * preact * (1.0 - tangent * tangent) * (
        gelu_scale + 3.0 * cubic_coef * gelu_scale * square
    )
    return (preact * half, slope_out)


def tile_of(size):
    for tile in (512, 384, 256, 128):
        if size % tile == 0:
            return tile
    return size


def plan(mesh_width, mesh_hidden, rows):
    hmaj = 4 if mesh_hidden % 4 == 0 else 1
    share = rows // mesh_hidden
    chunks = max(1, min(CHUNKS, share // 16))
    return hmaj, mesh_hidden // hmaj, chunks, share // chunks


def kernel(
    dims, x0_in, e2_in, st_own, t_own, wu_in, wd_in,
    xs_o, err_o, act_o, inn_o, gs_o,
    wu, wd, xs, err, act, inn, bk0, snd, rcv, own, yrc, hp, xr, zs, zr, gone,
    in_sem, out_sem, c1_s, c1_r, y_s, y_r, c3_s, c3_r,
    x_s, x_r, z_s, z_r, az_s, az_r, ax_s, ax_r,
):
    wide, hmaj, hmin, chunks, r = dims
    ysize = wide // 2
    rows, d = x0_in.shape
    f = wu_in.shape[1]
    fh = f // 2
    big = rows // chunks
    xrows = hmaj * r
    w = lax.axis_index("width")
    core, y = w % 2, w // 2
    h = lax.axis_index("hidden")
    hx, hz = h % hmin, h // hmin
    core_peer = {"width": y * 2 + 1 - core}

    def y_peer(j):
        return {"width": ((y + j) % ysize) * 2 + core}

    def x_pos(j):
        return (hx + j) % hmin

    def z_pos(j):
        return (hz + j) % hmaj

    def x_peer(j):
        return {"hidden": hz * hmin + x_pos(j)}

    def z_peer(j):
        return {"hidden": z_pos(j) * hmin + hx}

    loads = [
        pltpu.make_async_copy(src, dst, in_sem.at[i])
        for i, (src, dst) in enumerate(
            [
                (x0_in, xs.at[pl.ds(0, rows)]),
                (wu_in, wu),
                (wd_in, wd),
                (e2_in, err.at[pl.ds(rows, rows)]),
            ]
        )
    ]
    for load in loads:
        load.start()

    barrier = pltpu.get_barrier_semaphore()
    peers = [core_peer] + [y_peer(j) for j in range(1, ysize)]
    peers += [x_peer(j) for j in range(1, hmin)] + [z_peer(j) for j in range(1, hmaj)]
    for peer in peers:
        pl.semaphore_signal(barrier, inc=1, device_id=peer, device_id_type=pl.DeviceIdType.MESH)
    pl.semaphore_wait(barrier, len(peers))

    loaded = set()

    def need(*which):
        for i in which:
            if i not in loaded:
                loaded.add(i)
                loads[i].wait()

    inflight = {}

    def send(key, src, dst, ssem, rsem, peer):
        copy = pltpu.make_async_remote_copy(
            src_ref=src, dst_ref=dst, send_sem=ssem, recv_sem=rsem,
            device_id=peer, device_id_type=pl.DeviceIdType.MESH,
        )
        copy.start()
        inflight.setdefault(key, []).append(copy)

    def wait(key):
        for copy in inflight.pop(key, []):
            copy.wait()

    outs = []

    def put(src, dst):
        copy = pltpu.make_async_copy(src, dst, out_sem.at[len(outs)])
        copy.start()
        outs.append(copy)

    def put_wide(buf, out, first, count):
        for k in range(2):
            put(buf.at[k, pl.ds(first, count)], out.at[pl.ds(first, count), pl.ds(k * fh, fh)])

    ntile = tile_of(fh)
    dtile = tile_of(d)

    def half_matmul(lhs, lrow, weight, half, dst, row):
        def body(t, carry):
            col = pl.multiple_of(half * fh + t * ntile, 128)
            left = lhs[pl.ds(lrow, big), :]
            if weight == "up":
                prod = jnp.dot(left, wu[:, pl.ds(col, ntile)], preferred_element_type=F32)
            else:
                prod = lax.dot_general(left, wd[pl.ds(col, ntile), :], NT, preferred_element_type=F32)
            dst[pl.ds(row, big), pl.ds(pl.multiple_of(t * ntile, 128), ntile)] = prod.astype(BF16)
            return carry

        lax.fori_loop(0, fh // ntile, body, 0)

    lefts = [(xs, 0, "up"), (xs, rows, "up"), (err, rows, "down"), (err, 0, "down")]
    dests = [(inn, 0), (inn, rows), (act, rows), (bk0, 0)]
    sets = [0, 0, 1, 0]

    def w1(ar, c):
        lhs, base, weight = lefts[ar]
        need(*{0: (0, 1), 1: (), 2: (2, 3), 3: ()}[ar])
        if ar == 1:
            wait(("ax", 0, c))
            put(xs.at[pl.ds(rows + c * big, big)], xs_o.at[pl.ds(rows + c * big, big)])
        if ar == 3:
            wait(("ax", 1, c))
            put(err.at[pl.ds(c * big, big)], err_o.at[pl.ds(c * big, big)])
        s, row = sets[ar], c * big
        half_matmul(lhs, base + row, weight, 1 - core, snd.at[s], row)
        send(("c1", ar, c), snd.at[s, pl.ds(row, big)], rcv.at[s, pl.ds(row, big)],
             c1_s.at[ar, c], c1_r.at[ar, c], core_peer)
        half_matmul(lhs, base + row, weight, core, own.at[s], row)

    def row_loop(count, step, body):
        def wrapped(i, carry):
            body(pl.multiple_of(i * step, step))
            return carry

        lax.fori_loop(0, count // step, wrapped, 0)

    def w2(ar, c):
        s, row = sets[ar], c * big
        wait(("c1", ar, c))

        def body(i):
            at = pl.ds(row + i, 16)
            own[s, at] = (own[s, at].astype(F32) + rcv[s, at].astype(F32)).astype(BF16)

        row_loop(big, 16, body)
        dst, base = dests[ar]
        for j in range(1, ysize):
            if ysize == 2:
                target = dst.at[core, pl.ds(base + row, big)]
            else:
                target = yrc.at[ar * ysize + j, pl.ds(row, big)]
            send(("y", ar, c), own.at[s, pl.ds(row, big)], target,
                 y_s.at[ar, c, j], y_r.at[ar, c, j], y_peer(j))

    def w3(ar, c):
        s, row = sets[ar], c * big
        wait(("y", ar, c))
        dst, base = dests[ar]

        def body(i):
            at = pl.ds(row + i, 16)
            to = pl.ds(base + row + i, 16)
            total = own[s, at].astype(F32)
            for j in range(1, ysize):
                got = dst[core, to] if ysize == 2 else yrc[ar * ysize + j, at]
                total = total + got.astype(F32)
            dst[core, to] = total.astype(BF16)

        row_loop(big, 16, body)
        place = dst.at[core, pl.ds(base + row, big)]
        send(("c3", ar, c), place, place, c3_s.at[ar, c], c3_r.at[ar, c], core_peer)

    def h1(st, c):
        row = c * big
        wait(("c3", (0, 1, 3)[st], c))
        if st == 0:
            need(2)
        if st == 1:
            wait(("c3", 2, c))
        for k in range(2):
            def body(i):
                a = pl.ds(row + i, 16)
                b = pl.ds(rows + row + i, 16)
                if st == 0:
                    value, slope = gelu_parts(inn[k, a].astype(F32))
                    act[k, a] = value.astype(BF16)
                    inn[k, a] = slope.astype(BF16)
                elif st == 1:
                    value, slope = gelu_parts(inn[k, b].astype(F32))
                    back = act[k, b].astype(F32)
                    act[k, b] = value.astype(BF16)
                    inn[k, b] = (back * slope).astype(BF16)
                else:
                    inn[k, a] = (bk0[k, a].astype(F32) * inn[k, a].astype(F32)).astype(BF16)

            row_loop(big, 16, body)
        base = rows if st == 1 else 0

        def mm(t, carry):
            col = pl.ds(pl.multiple_of(t * dtile, 128), dtile)
            total = None
            for k in range(2):
                if st == 0:
                    prod = jnp.dot(act[k, pl.ds(row, big)], wd[pl.ds(k * fh, fh), col],
                                   preferred_element_type=F32)
                else:
                    prod = lax.dot_general(inn[k, pl.ds(base + row, big)], wu[col, pl.ds(k * fh, fh)],
                                           NT, preferred_element_type=F32)
                total = prod if total is None else total + prod
            hp[pl.ds(row, big), col] = total.astype(BF16)
            return carry

        lax.fori_loop(0, d // dtile, mm, 0)
        if st == 0:
            put_wide(act, act_o, row, big)
        elif st == 1:
            put_wide(act, act_o, rows + row, big)
            put_wide(inn, inn_o, rows + row, big)
        else:
            put_wide(inn, inn_o, row, big)
        for j in range(1, hmin):
            src = pl.ds(pl.multiple_of(row + x_pos(j) * xrows, 8), xrows)
            send(("x", st, c), hp.at[src], xr.at[j, pl.ds(c * xrows, xrows)],
                 x_s.at[st, c, j], x_r.at[st, c, j], x_peer(j))

    def h2(st, c):
        wait(("x", st, c))

        def body(i):
            at = pl.ds(c * xrows + i, 16)
            mine = pl.ds(pl.multiple_of(c * big + hx * xrows + i, 16), 16)
            total = hp[mine, :].astype(F32)
            for j in range(1, hmin):
                total = total + xr[j, at].astype(F32)
            zs[at] = total.astype(BF16)

        row_loop(xrows, 16, body)
        for j in range(1, hmaj):
            src = pl.ds(pl.multiple_of(c * xrows + z_pos(j) * r, 16), r)
            send(("z", st, c), zs.at[src], zr.at[j, pl.ds(c * r, r)],
                 z_s.at[st, c, j], z_r.at[st, c, j], z_peer(j))

    def share_place(st, c):
        buf, base = ((xs, rows), (err, 0))[st]
        return buf, base + c * big + hx * xrows

    def h3(st, c):
        wait(("z", st, c))
        for i in range(0, r, 16):
            at = pl.ds(c * r + i, 16)
            total = zs[pl.ds(pl.multiple_of(c * xrows + hz * r + i, 16), 16), :].astype(F32)
            for j in range(1, hmaj):
                total = total + zr[j, at].astype(F32)
            if st == 2:
                gs_o[at] = gone[at] + total
                continue
            total = total + (st_own, t_own)[st][at]
            if st == 1:
                gone[at] = total
            buf, first = share_place(st, c)
            buf[pl.ds(pl.multiple_of(first + hz * r + i, 16), 16), :] = total.astype(BF16)
        if st < 2:
            buf, first = share_place(st, c)
            place = buf.at[pl.ds(pl.multiple_of(first + hz * r, 16), r)]
            for j in range(1, hmaj):
                send(("az", st, c), place, place, az_s.at[st, c, j], az_r.at[st, c, j], z_peer(j))

    def h4(st, c):
        wait(("az", st, c))
        buf, first = share_place(st, c)
        place = buf.at[pl.ds(pl.multiple_of(first, 16), xrows)]
        for j in range(1, hmin):
            send(("ax", st, c), place, place, ax_s.at[st, c, j], ax_r.at[st, c, j], x_peer(j))

    need(0)
    put(xs.at[pl.ds(0, rows)], xs_o.at[pl.ds(0, rows)])
    chain = [
        (w1, 0), (w2, 0), (w3, 0), (h1, 0), (w1, 2), (h2, 0), (w2, 2), (h3, 0), (w3, 2), (h4, 0),
        (w1, 1), (w2, 1), (w3, 1), (h1, 1), (h2, 1), (h3, 1), (h4, 1),
        (w1, 3), (w2, 3), (w3, 3), (h1, 2), (h2, 2), (h3, 2),
    ]
    order = sorted(
        (i + c * OFFSET, c, i) for i in range(len(chain)) for c in range(chunks)
    )
    for _, c, i in order:
        step, arg = chain[i]
        step(arg, c)
    need(3)
    put(err.at[pl.ds(rows, rows)], err_o.at[pl.ds(rows, rows)])
    for copy in outs:
        copy.wait()


def shards(wide, hidden, start_latent, target_one, target_two, w_up, w_down):
    rows, d = start_latent.shape
    f = w_up.shape[1]
    hmaj, hmin, chunks, r = plan(wide, hidden, rows)
    share = rows // hidden
    ysize = wide // 2
    fh = f // 2
    xrows_all = rows // hmin

    def reorder(arr):
        cut = arr.astype(BF16).reshape(hmaj, hmin, chunks, r, d)
        return cut.transpose(2, 1, 0, 3, 4).reshape(rows, d)

    first = lax.axis_index("hidden") * share
    st_own = lax.dynamic_slice_in_dim(start_latent, first, share, 0)
    t_own = lax.dynamic_slice_in_dim(target_one, first, share, 0) + lax.dynamic_slice_in_dim(
        target_two, first, share, 0
    )
    vmem = pl.BlockSpec(memory_space=pltpu.VMEM)
    hbm = pl.BlockSpec(memory_space=pl.ANY)
    dma = pltpu.SemaphoreType.DMA
    yslots = 4 * ysize if ysize > 2 else 1
    yrows = rows if ysize > 2 else 16
    xs, err, act, inn, grad_start = pl.pallas_call(
        functools.partial(kernel, (wide, hmaj, hmin, chunks, r)),
        out_shape=(
            jax.ShapeDtypeStruct((2 * rows, d), BF16),
            jax.ShapeDtypeStruct((2 * rows, d), BF16),
            jax.ShapeDtypeStruct((2 * rows, f), BF16),
            jax.ShapeDtypeStruct((2 * rows, f), BF16),
            jax.ShapeDtypeStruct((share, d), F32),
        ),
        in_specs=[hbm, hbm, vmem, vmem, hbm, hbm],
        out_specs=[hbm, hbm, hbm, hbm, vmem],
        scratch_shapes=[
            pltpu.VMEM((d, f), BF16),
            pltpu.VMEM((f, d), BF16),
            pltpu.VMEM((2 * rows, d), BF16),
            pltpu.VMEM((2 * rows, d), BF16),
            pltpu.VMEM((2, 2 * rows, fh), BF16),
            pltpu.VMEM((2, 2 * rows, fh), BF16),
            pltpu.VMEM((2, rows, fh), BF16),
            pltpu.VMEM((2, rows, fh), BF16),
            pltpu.VMEM((2, rows, fh), BF16),
            pltpu.VMEM((2, rows, fh), BF16),
            pltpu.VMEM((yslots, yrows, fh if ysize > 2 else 128), BF16),
            pltpu.VMEM((rows, d), BF16),
            pltpu.VMEM((hmin, xrows_all, d), BF16),
            pltpu.VMEM((xrows_all, d), BF16),
            pltpu.VMEM((hmaj, share, d), BF16),
            pltpu.VMEM((share, d), F32),
            dma((4,)),
            dma((2 + 10 * chunks,)),
            dma((4, chunks)),
            dma((4, chunks)),
            dma((4, chunks, ysize)),
            dma((4, chunks, ysize)),
            dma((4, chunks)),
            dma((4, chunks)),
            dma((3, chunks, hmin)),
            dma((3, chunks, hmin)),
            dma((3, chunks, hmaj)),
            dma((3, chunks, hmaj)),
            dma((2, chunks, hmaj)),
            dma((2, chunks, hmaj)),
            dma((2, chunks, hmin)),
            dma((2, chunks, hmin)),
        ],
        compiler_params=pltpu.CompilerParams(
            collective_id=0, has_side_effects=True, vmem_limit_bytes=67043328
        ),
    )(reorder(start_latent), reorder(target_two), st_own, t_own, w_up, w_down)
    over_rows = (((0,), (0,)), ((), ()))
    grad_up = lax.dot_general(xs, inn, over_rows, preferred_element_type=F32)
    grad_down = lax.dot_general(act, err, over_rows, preferred_element_type=F32)
    return (grad_start, grad_up, grad_down)


def solution(mesh):
    return jax.shard_map(
        functools.partial(shards, mesh.shape["width"], mesh.shape["hidden"]),
        mesh=mesh,
        in_specs=(
            P(None, "width"),
            P(None, "width"),
            P(None, "width"),
            P("width", "hidden"),
            P("hidden", "width"),
        ),
        out_specs=(P("hidden", "width"), P("width", "hidden"), P("hidden", "width")),
        check_vma=False,
    )
```
